768 devices in a mesh: circ: 24 (over z, x_hi), radax: 32 (over y, x_lo, core).
Axes of the slice: x: 4 (x_hi: 2, x_lo: 2; x = x_hi * 2 + x_lo), y: 8, z: 12, core: 2. Of those that a mesh axis runs over, the one named last changes fastest.
Arguments:
- right_side: float32 [12288, 8192], P('circ', 'radax'), may hold values from -150 to 150
- coef_rotor: float32 [12288, 8192], P('circ', 'radax'), may hold values from 1.5 to 15
- coef_stator: float32 [12288, 8192], P('circ', 'radax'), may hold values from 1.5 to 15
- mortar_rows: int32 [12288], P('circ'), may hold values from 0 to 12287, as said below
- mortar_weight: float32 [12288], P('circ'), may hold values from 0.1 to 0.9
Outputs:
- solution_field: float32 [12288, 8192], P('circ', 'radax')
- residual: float32 [12288, 8192], P('circ', 'radax')
The draws below stay inside these ranges and needn't reach their ends.
Inputs may be any that keep to these rules, and one draw needn't show every extreme that they name: (mortar_rows[s] - s - 1280) taken modulo 12288 lies in -3 to 3, and both ends occur.
All inputs are finite; a program needn't handle non-finite values.
Results may differ from the reference program's by a relative error of at most 0.0002.
Values sent between devices are 32-bit elements; how exact they have to be, the bound alone decides.
A program may use at most 32 MiB of HBM per device.

```python
import math
import jax
import jax.numpy as jnp

W = 256
REACH = 3
SLIDE = 1280
NROWS = 12288
WG = 8192
N_RADAX = 32


def draw_right_side(key, part):
    key_noise = jax.random.fold_in(key, 11)
    key_rows = jax.random.fold_in(key, 12)
    key_cols = jax.random.fold_in(key, 13)
    row_scale = jnp.exp(jax.random.uniform(key_rows, (NROWS, 1), jnp.float32, 0.0, 2.302585))
    col_scale = jnp.exp(jax.random.uniform(key_cols, (1, WG), jnp.float32, 0.0, 2.302585))
    ramp = 1.0 + 2.0 * jnp.arange(NROWS, dtype=jnp.float32)[:, None] / NROWS
    noise = jax.random.truncated_normal(key_noise, -4.0, 4.0, (NROWS, WG), jnp.float32)
    return (0.1 * noise * row_scale * col_scale * ramp).astype(jnp.float32)


def draw_mortar_rows(key, part):
    key_delta = jax.random.fold_in(key, 21)
    delta = jax.random.randint(key_delta, (NROWS,), -REACH, REACH + 1, jnp.int32)
    delta = delta.at[0].set(-REACH).at[1].set(REACH)
    base = jnp.arange(NROWS, dtype=jnp.int32)
    return jnp.mod(base + SLIDE + delta, NROWS).astype(jnp.int32)


def levels(own_key, extent, shards, smallest, high):
    def one(position, blocks):
        draws = jax.random.uniform(jax.random.fold_in(jax.random.fold_in(own_key, 6), position), (blocks,), jnp.float32, smallest / len(shards), high / len(shards))
        return jnp.repeat(jnp.exp(draws), extent[position] // blocks).reshape((-1,) + (1,) * (len(extent) - position - 1))

    level = one(*shards[0])
    for cut in shards[1:]:
        level = level * one(*cut)
    return level


def setup_inputs(seed: int = 0) -> dict:
    keys = jax.random.split(jax.random.key(seed), 6)
    return {
        "right_side": draw_right_side(jax.random.fold_in(keys[5], 71), 0),
        "coef_rotor": jnp.clip(jnp.exp(math.log(15.0) - 2.3025851 * jax.random.uniform(keys[1], (NROWS, WG), jnp.float32) ** levels(keys[1], (NROWS, WG), ((0, 24), (1, 32)), -0.2, 0.2)), 1.5, 15.0),
        "coef_stator": jnp.clip(jnp.exp(math.log(15.0) - 2.3025851 * jax.random.uniform(keys[2], (NROWS, WG), jnp.float32) ** levels(keys[2], (NROWS, WG), ((0, 24), (1, 32)), -0.2, 0.2)), 1.5, 15.0),
        "mortar_rows": draw_mortar_rows(jax.random.fold_in(keys[5], 71), 0),
        "mortar_weight": jnp.clip(0.1 + 0.79999997 * jax.random.uniform(keys[4], (NROWS,), jnp.float32) ** levels(keys[4], (NROWS,), ((0, 24),), -0.2, 0.2), 0.1, 0.9),
    }


def stencil(grid_field, coef):
    above = jnp.roll(grid_field, 1, axis=0)
    below = jnp.roll(grid_field, -1, axis=0)
    blocks = grid_field.reshape(grid_field.shape[0], N_RADAX, W)
    padded = jnp.pad(blocks, ((0, 0), (0, 0), (1, 1)))
    beside = (padded[:, :, :-2] + padded[:, :, 2:]).reshape(grid_field.shape)
    return coef * grid_field - 0.25 * (above + below + beside)


def operator(trace, coef_rotor, coef_stator, first_rows, next_rows, weight):
    projected = weight * trace[first_rows] + (1.0 - weight) * trace[next_rows]
    response = stencil(projected, coef_stator)
    returned = jnp.zeros_like(trace).at[first_rows].add(weight * response)
    returned = returned.at[next_rows].add((1.0 - weight) * response)
    return stencil(trace, coef_rotor) + returned


def reference(right_side, coef_rotor, coef_stator, mortar_rows, mortar_weight):
    first_rows = mortar_rows.astype(jnp.int32)
    next_rows = jnp.mod(first_rows + 1, NROWS).astype(jnp.int32)
    weight = mortar_weight[:, None]
    image = operator(right_side, coef_rotor, coef_stator, first_rows, next_rows, weight)
    second = operator(image, coef_rotor, coef_stator, first_rows, next_rows, weight)
    cross_one = jnp.sum(right_side * image)
    cross_two = jnp.sum(right_side * second)
    gram_pp = jnp.sum(image * image)
    gram_pq = jnp.sum(image * second)
    gram_qq = jnp.sum(second * second)
    determinant = gram_pp * gram_qq - gram_pq * gram_pq
    coeff_one = (gram_qq * cross_one - gram_pq * cross_two) / determinant
    coeff_two = (gram_pp * cross_two - gram_pq * cross_one) / determinant
    solution_field = coeff_one * right_side + coeff_two * image
    residual = right_side - coeff_one * image - coeff_two * second
    return solution_field, residual
```

```python
import jax
import jax.numpy as jnp
from jax import lax
from jax.experimental import pallas as pl
from jax.experimental.pallas import tpu as pltpu
from jax.sharding import Mesh
from jax.sharding import PartitionSpec as P

AXES = ("z", "xh", "y", "xl", "core")
SIZES = (12, 2, 8, 2, 2)
CIRC = 24
ROWS = 512
W = 256
NROWS = CIRC * ROWS
PAD = 8
EXT = 544
MESH = pl.DeviceIdType.MESH
HIGH = lax.Precision.HIGHEST

CHUNKS = (
    [(0, 16, 0, 24)]
    + [(16 + 128 * k, 128, 8 + 128 * k, 144) for k in range(4)]
    + [(528, 16, 520, 24)]
)
X_PARTNERS = [(0, a, 0, b, k) for a in range(2) for b in range(2) for k in range(2) if a + b + k]
Y_PARTNERS = [(0, 0, d, 0, 0) for d in range(1, 8)]
Z_PARTNERS = [(d, 0, 0, 0, 0) for d in range(1, 12)]
EXTRA = [(d, 1, 0, 0, 0) for d in (1, 2, 10, 11)]


def kernel(r_in, cr_in, cs_in, m_in, w_in, image_out, second_out, y_out,
           u, cr, cs, v, im, se, m3, m2, w3, w2, pt_big, p_big, pt_small, p_small,
           mine, from_x, from_y, from_z, local_sem, send_sem, recv_sem, ar_send, ar_recv, out_sem):
    me = [lax.axis_index(a) for a in AXES]
    circ = me[0] * 2 + me[1]

    def along(shift):
        c = lax.rem(circ + (shift + CIRC), CIRC)
        return (lax.div(c, 2), lax.rem(c, 2), me[2], me[3], me[4])

    def at(offset):
        return tuple(lax.rem(p + o, n) if o else p for p, o, n in zip(me, offset, SIZES))

    barrier = pltpu.get_barrier_semaphore()
    greeted = X_PARTNERS + Y_PARTNERS + Z_PARTNERS + EXTRA
    for offset in greeted:
        pl.semaphore_signal(barrier, inc=1, device_id=at(offset), device_id_type=MESH)
    own = [
        pltpu.make_async_copy(r_in, u.at[pl.ds(PAD + 16, ROWS)], local_sem.at[0]),
        pltpu.make_async_copy(cr_in, cr.at[pl.ds(PAD + 16, ROWS)], local_sem.at[1]),
    ]
    for copy in own:
        copy.start()
    nothing = jnp.zeros((PAD, W), jnp.float32)
    for ref in (u, v):
        ref[0:PAD] = nothing
        ref[PAD + EXT : PAD + EXT + PAD] = nothing
    for ref in (im, se):
        ref[...] = jnp.zeros(ref.shape, jnp.float32)
    pl.semaphore_wait(barrier, len(greeted))

    def send(i, src, dst, shift):
        return pltpu.make_async_remote_copy(
            src_ref=src, dst_ref=dst, send_sem=send_sem.at[i], recv_sem=recv_sem.at[i],
            device_id=along(shift), device_id_type=MESH)

    small = [
        send(0, m_in, m3, 3), send(1, w_in, w3, 3), send(2, m_in, m2, 2), send(3, w_in, w2, 2),
        send(4, r_in.at[pl.ds(0, 16)], u.at[pl.ds(PAD + 528, 16)], -1),
        send(5, r_in.at[pl.ds(496, 16)], u.at[pl.ds(PAD, 16)], 1),
        send(6, cr_in.at[pl.ds(0, 8)], cr.at[pl.ds(PAD + 528, 8)], -1),
        send(7, cr_in.at[pl.ds(504, 8)], cr.at[pl.ds(PAD + 8, 8)], 1),
    ]
    bulk = [
        send(8, cs_in.at[pl.ds(240, 144)], cs.at[pl.ds(PAD + 0, 144)], 3),
        send(9, cs_in.at[pl.ds(384, 128)], cs.at[pl.ds(PAD + 144, 128)], 3),
        send(10, cs_in.at[pl.ds(0, 128)], cs.at[pl.ds(PAD + 272, 128)], 2),
        send(11, cs_in.at[pl.ds(128, 144)], cs.at[pl.ds(PAD + 400, 144)], 2),
    ]
    for copy in small + bulk:
        copy.start()

    col = lax.broadcasted_iota(jnp.int32, (1, W), 1)
    not_first = col > 0
    not_last = col < W - 1

    def around(ref, start, count):
        mid = ref[pl.ds(start, count)]
        beside = (jnp.where(not_first, pltpu.roll(mid, 1, 1), 0.0)
                  + jnp.where(not_last, pltpu.roll(mid, W - 1, 1), 0.0))
        return mid, 0.25 * (ref[pl.ds(start - 1, count)] + ref[pl.ds(start + 1, count)] + beside)

    for copy in small[:4]:
        copy.wait()
    base = circ * ROWS - 16
    eye = jnp.where(lax.broadcasted_iota(jnp.int32, (128, 128), 0)
                    == lax.broadcasted_iota(jnp.int32, (128, 128), 1), 1.0, 0.0).astype(jnp.float32)

    def mortar(rows, weights, first, count, lanes):
        place = rows - base
        place = jnp.where(place < 0, place + NROWS, place)
        place = jnp.where(place >= NROWS, place - NROWS, place)
        line = lax.broadcasted_iota(jnp.int32, (count, lanes), 0) + first
        return jnp.where(line == place, weights, 0.0) + jnp.where(line == place + 1, 1.0 - weights, 0.0)

    def lanes16(row, roll):
        return (pltpu.roll(row, roll, 1) if roll else row)[:, :16]

    sources = [(m3, w3, 2), (m3, w3, 3), (m2, w2, 0), (m2, w2, 1)]
    for k, (m, w, line) in enumerate(sources):
        pt = mortar(m[line : line + 1, :], w[line : line + 1, :], 8 + 128 * k, 144, 128)
        pt_big[k] = pt
        p_big[k] = lax.dot_general(eye, pt, (((1,), (1,)), ((), ())), precision=HIGH,
                                   preferred_element_type=jnp.float32)
    for k, (m, w, line, roll, first) in enumerate([(m3, w3, 1, 16, 0), (m2, w2, 2, 0, 520)]):
        pt = mortar(lanes16(m[line : line + 1, :], roll), lanes16(w[line : line + 1, :], roll), first, 24, 16)
        pt_small[k] = pt
        p_small[k] = lax.dot_general(eye[:16, :16], pt, (((1,), (1,)), ((), ())), precision=HIGH,
                                     preferred_element_type=jnp.float32)

    def matrices(i):
        if i == 0 or i == 5:
            return p_small[i // 5], pt_small[i // 5]
        return p_big[i - 1], pt_big[i - 1]

    def project(ref):
        for i, (first, count, rotor, rotor_count) in enumerate(CHUNKS):
            v[pl.ds(PAD + first, count)] = jnp.dot(
                matrices(i)[0], ref[pl.ds(PAD + rotor, rotor_count)], precision=HIGH,
                preferred_element_type=jnp.float32)

    def give_back(ref, i):
        first, count, rotor, rotor_count = CHUNKS[i]
        mid, rest = around(v, PAD + first, count)
        response = cs[pl.ds(PAD + first, count)] * mid - rest
        ref[pl.ds(PAD + rotor, rotor_count)] += jnp.dot(
            matrices(i)[1], response, precision=HIGH, preferred_element_type=jnp.float32)

    def rotor_part(ref, out, start, count):
        mid, rest = around(ref, start, count)
        out[pl.ds(start, count)] = cr[pl.ds(start, count)] * mid - rest

    for copy in own:
        copy.wait()
    for copy in small[4:]:
        copy.wait()
    project(u)
    for q in range(4):
        rotor_part(u, im, PAD + 8 + 132 * q + 4 * (q % 2), 136 if q % 2 == 0 else 128)
    bulk[0].wait()
    give_back(im, 0)
    give_back(im, 1)
    bulk[1].wait()
    give_back(im, 2)
    bulk[2].wait()
    give_back(im, 3)
    bulk[3].wait()
    give_back(im, 4)
    give_back(im, 5)
    image_copy = pltpu.make_async_copy(im.at[pl.ds(PAD + 16, ROWS)], image_out, out_sem.at[0])
    project(im)
    for q in range(4):
        rotor_part(im, se, PAD + 16 + 128 * q, 128)
    for i in range(6):
        give_back(se, i)
    image_copy.start()
    second_copy = pltpu.make_async_copy(se.at[pl.ds(PAD + 16, ROWS)], second_out, out_sem.at[1])

    parts = [jnp.zeros((8, W), jnp.float32)] * 5
    for q in range(8):
        at_rows = pl.ds(PAD + 16 + 64 * q, 64)
        b, p, s = u[at_rows], im[at_rows], se[at_rows]
        for n, product in enumerate((b * p, b * s, p * p, p * s, s * s)):
            parts[n] = parts[n] + jnp.sum(product.reshape(8, 8, W), axis=0)
    lane = lax.broadcasted_iota(jnp.int32, (1, 128), 1)
    total = jnp.zeros((1, 128), jnp.float32)
    for n, part in enumerate(parts):
        total = jnp.where(lane == n, jnp.sum(part), total)
    second_copy.start()

    done = 0
    for stage, (partners, got) in enumerate(((X_PARTNERS, from_x), (Y_PARTNERS, from_y), (Z_PARTNERS, from_z))):
        mine[stage] = total
        copies = [
            pltpu.make_async_remote_copy(
                src_ref=mine.at[stage], dst_ref=got.at[pl.ds(n, 1)],
                send_sem=ar_send.at[done + n], recv_sem=ar_recv.at[done + n],
                device_id=at(offset), device_id_type=MESH)
            for n, offset in enumerate(partners)
        ]
        done += len(partners)
        for copy in copies:
            copy.start()
        for copy in copies:
            copy.wait()
        total = total + jnp.sum(got[0 : len(partners)], axis=0, keepdims=True)

    def pick(n):
        return jnp.sum(jnp.where(lane == n, total, 0.0), axis=1, keepdims=True)

    cross_one, cross_two, gram_pp, gram_pq, gram_qq = [pick(n) for n in range(5)]
    determinant = gram_pp * gram_qq - gram_pq * gram_pq
    y1 = (gram_qq * cross_one - gram_pq * cross_two) / determinant
    y2 = (gram_pp * cross_two - gram_pq * cross_one) / determinant
    y_out[0:8] = jnp.broadcast_to(y1, (8, W))
    y_out[8:16] = jnp.broadcast_to(y2, (8, W))
    image_copy.wait()
    second_copy.wait()


def local(right_side, coef_rotor, coef_stator, mortar_rows, mortar_weight):
    f32 = jnp.float32
    block = jax.ShapeDtypeStruct((ROWS, W), f32)
    wide = pltpu.VMEM((PAD + EXT + PAD, W), f32)
    hbm = pl.BlockSpec(memory_space=pl.ANY)
    image, second, y = pl.pallas_call(
        kernel,
        out_shape=(block, block, jax.ShapeDtypeStruct((16, W), f32)),
        in_specs=[hbm] * 5,
        out_specs=(hbm, hbm, pl.BlockSpec(memory_space=pltpu.VMEM)),
        scratch_shapes=[wide] * 6
        + [pltpu.VMEM((4, 128), jnp.int32)] * 2
        + [pltpu.VMEM((4, 128), f32)] * 2
        + [
            pltpu.VMEM((4, 144, 128), f32),
            pltpu.VMEM((4, 128, 144), f32),
            pltpu.VMEM((2, 24, 16), f32),
            pltpu.VMEM((2, 16, 24), f32),
            pltpu.VMEM((3, 1, 128), f32),
            pltpu.VMEM((8, 128), f32),
            pltpu.VMEM((8, 128), f32),
            pltpu.VMEM((16, 128), f32),
            pltpu.SemaphoreType.DMA((2,)),
            pltpu.SemaphoreType.DMA((12,)),
            pltpu.SemaphoreType.DMA((12,)),
            pltpu.SemaphoreType.DMA((25,)),
            pltpu.SemaphoreType.DMA((25,)),
            pltpu.SemaphoreType.DMA((2,)),
        ],
        compiler_params=pltpu.CompilerParams(collective_id=0, has_side_effects=True),
    )(right_side, coef_rotor, coef_stator, mortar_rows.reshape(4, 128), mortar_weight.reshape(4, 128))
    y1, y2 = y[0:1], y[8:9]
    return y1 * right_side + y2 * image, right_side - y1 * image - y2 * second


def solution(mesh):
    finer = Mesh(mesh.devices.reshape(SIZES), AXES)
    circ, radax = AXES[:2], AXES[2:]
    whole = P(circ, radax)
    return jax.shard_map(local, mesh=finer, in_specs=(whole, whole, whole, P(circ), P(circ)),
                         out_specs=(whole, whole), check_vma=False)
```

```python
import jax
import jax.numpy as jnp
from jax import lax
from jax.experimental import pallas as pl
from jax.experimental.pallas import tpu as pltpu
from jax.sharding import Mesh
from jax.sharding import PartitionSpec as P

AXES = ("z", "xh", "y", "xl", "core")
SIZES = (12, 2, 8, 2, 2)
CIRC = 24
ROWS = 512
W = 256
NROWS = CIRC * ROWS
PAD = 8
EXT = 544
CUT = 272
HELP = 272
MESH = pl.DeviceIdType.MESH
HIGH = lax.Precision.HIGHEST
F32 = jnp.float32

FRONT = [(0, 16, 3, 1, 112), (16, 128, 3, 2, 0), (144, 128, 3, 3, 0), (272, 32, 2, 0, 0)]
BACK = [(304, 96, 2, 0, 32), (400, 128, 2, 1, 0), (528, 16, 2, 2, 0)]
OWN = [(0, 128, 0, 0, 0), (128, 128, 0, 1, 0), (256, 16, 0, 2, 0)]
X_PARTNERS = [(0, a, 0, b, k) for a in range(2) for b in range(2) for k in range(2) if a + b + k]
Y_PARTNERS = [(0, 0, d, 0, 0) for d in range(1, 8)]
Z_PARTNERS = [(d, 0, 0, 0, 0) for d in range(1, 12)]
NEAR = [(d, a, 0, 0, 0) for d in (1, 2, 10, 11) for a in range(2)]
N_SENDS = 16


def window(piece, size):
    low = max(piece[0] - 8, 0)
    return low, min(piece[0] + piece[1] + 8, size) - low


SHAPES = [(window(p, EXT)[1], p[1]) for p in FRONT + BACK] + [(window(p, HELP)[1], p[1]) for p in OWN]


def kernel(r_in, cr_in, cs_in, m_in, w_in, image_out, second_out, y1_out, y2_out,
           u, cr, cs, v, v2, im, se, se2, uh, crh, csh, vh, vh2, imh, seh,
           m3, m2, m0, w3, w2, w0, mine, from_x, from_y, from_z,
           local_sem, send_sem, recv_sem, ar_send, ar_recv, token, *matrices):
    me = [lax.axis_index(a) for a in AXES]
    circ = me[0] * 2 + me[1]
    count = len(SHAPES)
    give, take = matrices[:count], matrices[count:]

    def along(shift):
        c = lax.rem(circ + (shift + CIRC), CIRC)
        return (lax.div(c, 2), lax.rem(c, 2), me[2], me[3], me[4])

    def at(offset):
        return tuple(lax.rem(p + o, n) if o else p for p, o, n in zip(me, offset, SIZES))

    barrier = pltpu.get_barrier_semaphore()
    greeted = X_PARTNERS + Y_PARTNERS + NEAR
    for offset in greeted:
        pl.semaphore_signal(barrier, inc=1, device_id=at(offset), device_id_type=MESH)
    own = [
        pltpu.make_async_copy(m_in, m0, local_sem.at[0]),
        pltpu.make_async_copy(w_in, w0, local_sem.at[1]),
        pltpu.make_async_copy(r_in, u.at[pl.ds(PAD + 16, ROWS)], local_sem.at[2]),
        pltpu.make_async_copy(cr_in, cr.at[pl.ds(PAD + 16, ROWS)], local_sem.at[3]),
        pltpu.make_async_copy(cs_in.at[pl.ds(0, HELP)], csh.at[pl.ds(PAD, HELP)], local_sem.at[4]),
    ]
    for copy in own:
        copy.start()

    def send(i, src, dst, shift):
        return pltpu.make_async_remote_copy(
            src_ref=src, dst_ref=dst, send_sem=send_sem.at[i], recv_sem=recv_sem.at[i],
            device_id=along(shift), device_id_type=MESH)

    def rows(ref, first, n):
        return ref.at[pl.ds(first, n)]

    mortar_sends = [send(0, m_in, m3, 3), send(1, w_in, w3, 3), send(2, m_in, m2, 2), send(3, w_in, w2, 2)]
    halo_sends = [
        send(4, rows(r_in, 0, 16), rows(u, PAD + 528, 16), -1),
        send(5, rows(r_in, 496, 16), rows(u, PAD, 16), 1),
        send(6, rows(cr_in, 0, 8), rows(cr, PAD + 528, 8), -1),
        send(7, rows(cr_in, 504, 8), rows(cr, PAD + 8, 8), 1),
    ]
    help_r = [send(8, rows(r_in, 0, 16), rows(uh, PAD + 256, 16), -3),
              send(9, rows(r_in, 256, 256), rows(uh, PAD, 256), -2)]
    help_cr = [send(10, rows(cr_in, 0, 8), rows(crh, PAD + 256, 8), -3),
               send(11, rows(cr_in, 264, 248), rows(crh, PAD + 8, 248), -2)]
    front = [send(12, rows(cs_in, 240, 144), rows(cs, PAD, 144), 3),
             send(13, rows(cs_in, 384, 128), rows(cs, PAD + 144, 128), 3),
             send(14, rows(cs_in, 0, 32), rows(cs, PAD + 272, 32), 2)]
    back = send(15, rows(cs_in, 32, 240), rows(cs, PAD + 304, 240), 2)
    sends = mortar_sends + halo_sends + [help_r[0], help_cr[0], help_r[1], front[2], front[0], front[1], help_cr[1], back]

    nothing = jnp.zeros((PAD, W), F32)
    for ref, size in ((u, EXT), (v, EXT), (v2, EXT), (uh, HELP), (vh, HELP), (vh2, HELP)):
        ref[0:PAD] = nothing
        ref[PAD + size : PAD + size + PAD] = nothing
    for ref in (im, se, se2, imh, seh):
        ref[...] = jnp.zeros(ref.shape, F32)

    eye = jnp.where(lax.broadcasted_iota(jnp.int32, (128, 128), 0)
                    == lax.broadcasted_iota(jnp.int32, (128, 128), 1), 1.0, 0.0).astype(F32)

    def mortar(index, piece, size, base, m, w):
        _, n, _, line, place = piece
        low, span = window(piece, size)

        def lanes(ref):
            row = ref[line : line + 1, :]
            return (pltpu.roll(row, 128 - place, 1) if place else row)[:, :n]

        spot, weights = lanes(m) - base, lanes(w)
        spot = jnp.where(spot < 0, spot + NROWS, spot)
        spot = jnp.where(spot >= NROWS, spot - NROWS, spot)
        row = lax.broadcasted_iota(jnp.int32, (span, n), 0) + low
        pt = jnp.where(row == spot, weights, 0.0) + jnp.where(row == spot + 1, 1.0 - weights, 0.0)
        give[index][...] = pt
        take[index][...] = lax.dot_general(eye[:n, :n], pt, (((1,), (1,)), ((), ())), precision=HIGH,
                                           preferred_element_type=F32)

    own[0].wait()
    own[1].wait()
    for n, piece in enumerate(OWN):
        mortar(7 + n, piece, HELP, lax.rem(circ * ROWS + 1280, NROWS), m0, w0)
    pl.semaphore_wait(barrier, len(greeted))
    for copy in sends:
        copy.start()

    def spread(n):
        for offset in ((2, 0, 0, 0, 0), (10, 0, 0, 0, 0)):
            pl.semaphore_signal(token.at[n], inc=1, device_id=at(offset), device_id_type=MESH)

    spread(0)

    col = lax.broadcasted_iota(jnp.int32, (1, W), 1)
    not_first = col > 0
    not_last = col < W - 1

    def around(ref, start, n):
        mid = ref[pl.ds(start, n)]
        beside = (jnp.where(not_first, pltpu.roll(mid, 1, 1), 0.0)
                  + jnp.where(not_last, pltpu.roll(mid, W - 1, 1), 0.0))
        return mid, 0.25 * (ref[pl.ds(start - 1, n)] + ref[pl.ds(start + 1, n)] + beside)

    def project(src, dst, index, piece, size):
        low, span = window(piece, size)
        dst[pl.ds(PAD + piece[0], piece[1])] = jnp.dot(
            take[index][...], src[pl.ds(PAD + low, span)], precision=HIGH, preferred_element_type=F32)

    def give_back(src, coef, dst, index, piece, size):
        low, span = window(piece, size)
        mid, rest = around(src, PAD + piece[0], piece[1])
        response = coef[pl.ds(PAD + piece[0], piece[1])] * mid - rest
        dst[pl.ds(PAD + low, span)] += jnp.dot(
            give[index][...], response, precision=HIGH, preferred_element_type=F32)

    def rotor_part(src, coef, dst, first, end):
        for start in range(first, end, 128):
            n = min(128, end - start)
            mid, rest = around(src, PAD + start, n)
            dst[pl.ds(PAD + start, n)] += coef[pl.ds(PAD + start, n)] * mid - rest

    def add_products(parts, b_ref, p_ref, s_ref, first, end):
        for start in range(first, end, 16):
            at_rows = pl.ds(PAD + start, 16)
            b, p, s = b_ref[at_rows], p_ref[at_rows], s_ref[at_rows]
            for n, product in enumerate((b * p, b * s, p * p, p * s, s * s)):
                parts[n] = parts[n] + (product[:8] + product[8:])
        return parts

    pl.semaphore_wait(token.at[0], 2)
    spread(1)
    for copy in mortar_sends:
        copy.wait_recv()
    base = circ * ROWS - 16
    for n, piece in enumerate(FRONT + BACK):
        mortar(n, piece, EXT, base, *((m3, w3) if piece[2] == 3 else (m2, w2)))
    for copy in own[2:]:
        copy.wait()
    for copy in halo_sends:
        copy.wait_recv()
    for n, piece in enumerate(FRONT + BACK):
        project(u, v, n, piece, EXT)
    rotor_part(u, cr, im, 8, 536)

    pl.semaphore_wait(token.at[1], 2)
    for copy in help_r:
        copy.wait_recv()
    for n, piece in enumerate(OWN):
        project(uh, vh, 7 + n, piece, HELP)
    for n, piece in enumerate(OWN):
        give_back(vh, csh, imh, 7 + n, piece, HELP)

    for copy in help_cr:
        copy.wait_recv()
    rotor_part(uh, crh, imh, 8, 264)
    for n, piece in enumerate(OWN):
        project(imh, vh2, 7 + n, piece, HELP)
    rotor_part(imh, crh, seh, 16, 256)
    for n, piece in enumerate(OWN):
        give_back(vh2, csh, seh, 7 + n, piece, HELP)
    parts = add_products([jnp.zeros((8, W), F32)] * 5, uh, imh, seh, 16, 256)

    front[2].wait_recv()
    give_back(v, cs, im, 3, FRONT[3], EXT)
    front[0].wait_recv()
    give_back(v, cs, im, 0, FRONT[0], EXT)
    give_back(v, cs, im, 1, FRONT[1], EXT)
    front[1].wait_recv()
    give_back(v, cs, im, 2, FRONT[2], EXT)
    for n, piece in enumerate(FRONT):
        project(im, v2, n, piece, EXT)
    rotor_part(im, cr, se, 16, 16 + CUT)
    for n, piece in enumerate(FRONT):
        give_back(v2, cs, se, n, piece, EXT)
    parts = add_products(parts, u, im, se, 16, 16 + CUT)

    lane = lax.broadcasted_iota(jnp.int32, (1, 128), 1)
    total = jnp.zeros((1, 128), F32)
    for n, part in enumerate(parts):
        line = jnp.sum(part[:, :128] + part[:, 128:], axis=0, keepdims=True)
        total = jnp.where(lane == n, jnp.sum(line, axis=1, keepdims=True), total)

    def late():
        back.wait_recv()
        for n, piece in enumerate(BACK):
            give_back(v, cs, im, 4 + n, piece, EXT)
        for n, piece in list(enumerate(FRONT + BACK))[3:]:
            project(im, v2, n, piece, EXT)
        rotor_part(im, cr, se2, 16 + CUT, 528)
        for n, piece in list(enumerate(FRONT + BACK))[3:]:
            give_back(v2, cs, se2, n, piece, EXT)
        image_out[...] = im[PAD + 16 : PAD + 528]
        second_out[:CUT] = se[PAD + 16 : PAD + 16 + CUT]
        second_out[CUT:] = se2[PAD + 16 + CUT : PAD + 528]

    done = 0
    for stage, (partners, got) in enumerate(((X_PARTNERS, from_x), (Y_PARTNERS, from_y), (Z_PARTNERS, from_z))):
        mine[stage] = total
        copies = [
            pltpu.make_async_remote_copy(
                src_ref=mine.at[stage], dst_ref=got.at[pl.ds(n, 1)],
                send_sem=ar_send.at[done + n], recv_sem=ar_recv.at[done + n],
                device_id=at(offset), device_id_type=MESH)
            for n, offset in enumerate(partners)
        ]
        done += len(partners)
        for copy in copies:
            copy.start()
        if stage == 2:
            late()
        for copy in copies:
            copy.wait()
        total = total + jnp.sum(got[0 : len(partners)], axis=0, keepdims=True)

    def pick(n):
        return jnp.sum(jnp.where(lane == n, total, 0.0), axis=1, keepdims=True)

    cross_one, cross_two, gram_pp, gram_pq, gram_qq = [pick(n) for n in range(5)]
    determinant = gram_pp * gram_qq - gram_pq * gram_pq
    y1 = (gram_qq * cross_one - gram_pq * cross_two) / determinant
    y2 = (gram_pp * cross_two - gram_pq * cross_one) / determinant
    y1_out[...] = jnp.broadcast_to(y1, (1, W))
    y2_out[...] = jnp.broadcast_to(y2, (1, W))
    for copy in sends:
        copy.wait_send()


def local(right_side, coef_rotor, coef_stator, mortar_rows, mortar_weight):
    main = pltpu.VMEM((PAD + EXT + PAD, W), F32)
    helper = pltpu.VMEM((PAD + HELP + PAD, W), F32)
    hbm = pl.BlockSpec(memory_space=pltpu.HBM)
    vmem = pl.BlockSpec(memory_space=pltpu.VMEM)
    image, second, y1, y2 = pl.pallas_call(
        kernel,
        out_shape=(pltpu.VMEM((ROWS, W), F32), pltpu.VMEM((ROWS, W), F32), pltpu.VMEM((1, W), F32), pltpu.VMEM((1, W), F32)),
        in_specs=[hbm] * 5,
        out_specs=(vmem,) * 4,
        scratch_shapes=[main] * 8
        + [helper] * 7
        + [pltpu.VMEM((4, 128), jnp.int32)] * 3
        + [pltpu.VMEM((4, 128), F32)] * 3
        + [pltpu.VMEM((3, 1, 128), F32), pltpu.VMEM((8, 128), F32), pltpu.VMEM((8, 128), F32), pltpu.VMEM((16, 128), F32)]
        + [pltpu.SemaphoreType.DMA((n,)) for n in (5, N_SENDS, N_SENDS, 25, 25)]
        + [pltpu.SemaphoreType.REGULAR((2,))]
        + [pltpu.VMEM(s, F32) for s in SHAPES]
        + [pltpu.VMEM(s[::-1], F32) for s in SHAPES],
        compiler_params=pltpu.CompilerParams(collective_id=0, has_side_effects=True),
    )(right_side, coef_rotor, coef_stator, mortar_rows.reshape(4, 128), mortar_weight.reshape(4, 128))
    return y1 * right_side + y2 * image, right_side - y1 * image - y2 * second


def solution(mesh):
    finer = Mesh(mesh.devices.reshape(SIZES), AXES)
    circ, radax = AXES[:2], AXES[2:]
    whole = P(circ, radax)
    return jax.shard_map(local, mesh=finer, in_specs=(whole, whole, whole, P(circ), P(circ)),
                         out_specs=(whole, whole), check_vma=False)
```

```python
import jax
import jax.numpy as jnp
from jax import lax
from jax.experimental import pallas as pl
from jax.experimental.pallas import tpu as pltpu
from jax.sharding import Mesh
from jax.sharding import PartitionSpec as P

AXES = ("z", "xh", "y", "xl", "core")
SIZES = (12, 2, 8, 2, 2)
CIRC = 24
ROWS = 512
W = 256
NROWS = CIRC * ROWS
PAD = 8
EXT = 544
CUT = 296
HELP = 248
RELAY = 64
MESH = pl.DeviceIdType.MESH
HIGH = lax.Precision.HIGHEST
F32 = jnp.float32

FRONT = [(0, 16, 3, 1, 112), (16, 128, 3, 2, 0), (144, 16, 3, 3, 0), (160, 112, 3, 3, 16), (272, 56, 2, 0, 0)]
BACK = [(328, 72, 2, 0, 56), (400, 128, 2, 1, 0), (528, 16, 2, 2, 0)]
OWN = [(0, 104, 0, 0, 24), (104, 128, 0, 1, 0), (232, 16, 0, 2, 0)]
X_PARTNERS = [(0, a, 0, b, k) for a in range(2) for b in range(2) for k in range(2) if a + b + k]
Y_PARTNERS = [(0, 0, d, 0, 0) for d in range(1, 8)]
Z_PARTNERS = [(d, 0, 0, 0, 0) for d in range(1, 12)]
NEAR = [(d, a, 0, 0, 0) for d in (1, 2, 10, 11) for a in range(2)]
N_SENDS = 18
FIRST_BACK = len(FRONT)
FIRST_OWN = len(FRONT + BACK)


def window(piece, size):
    low = max(piece[0] - 8, 0)
    return low, min(piece[0] + piece[1] + 8, size) - low


SHAPES = [(window(p, EXT)[1], p[1]) for p in FRONT + BACK] + [(window(p, HELP)[1], p[1]) for p in OWN]


def kernel(r_in, cr_in, cs_in, m_in, w_in, image_out, second_out, y1_out, y2_out,
           u, cr, cs, v, v2, im, se, se2, uh, crh, csh, vh, vh2, imh, seh,
           relay, m3, m2, m0, w3, w2, w0, mine, from_x, from_y, from_z,
           local_sem, send_sem, recv_sem, ar_send, ar_recv, token, *matrices):
    me = [lax.axis_index(a) for a in AXES]
    circ = me[0] * 2 + me[1]
    count = len(SHAPES)
    give, take = matrices[:count], matrices[count:]

    def along(shift):
        c = lax.rem(circ + (shift + CIRC), CIRC)
        return (lax.div(c, 2), lax.rem(c, 2), me[2], me[3], me[4])

    def at(offset):
        return tuple(lax.rem(p + o, n) if o else p for p, o, n in zip(me, offset, SIZES))

    barrier = pltpu.get_barrier_semaphore()
    greeted = X_PARTNERS + Y_PARTNERS + NEAR
    for offset in greeted:
        pl.semaphore_signal(barrier, inc=1, device_id=at(offset), device_id_type=MESH)
    own = [
        pltpu.make_async_copy(m_in, m0, local_sem.at[0]),
        pltpu.make_async_copy(w_in, w0, local_sem.at[1]),
        pltpu.make_async_copy(r_in, u.at[pl.ds(PAD + 16, ROWS)], local_sem.at[2]),
        pltpu.make_async_copy(cr_in, cr.at[pl.ds(PAD + 16, ROWS)], local_sem.at[3]),
        pltpu.make_async_copy(cs_in.at[pl.ds(24, HELP)], csh.at[pl.ds(PAD, HELP)], local_sem.at[4]),
    ]
    for copy in own:
        copy.start()

    def send(i, src, dst, shift):
        return pltpu.make_async_remote_copy(
            src_ref=src, dst_ref=dst, send_sem=send_sem.at[i], recv_sem=recv_sem.at[i],
            device_id=along(shift), device_id_type=MESH)

    def rows(ref, first, n):
        return ref.at[pl.ds(first, n)]

    mortar_sends = [send(0, m_in, m3, 3), send(1, w_in, w3, 3), send(2, m_in, m2, 2), send(3, w_in, w2, 2)]
    halo_sends = [
        send(4, rows(r_in, 0, 16), rows(u, PAD + 528, 16), -1),
        send(5, rows(r_in, 496, 16), rows(u, PAD, 16), 1),
        send(6, rows(cr_in, 0, 8), rows(cr, PAD + 528, 8), -1),
        send(7, rows(cr_in, 504, 8), rows(cr, PAD + 8, 8), 1),
    ]
    help_r = [send(8, rows(r_in, 0, 16), rows(uh, PAD + 232, 16), -3),
              send(9, rows(r_in, 280, 232), rows(uh, PAD, 232), -2)]
    help_cr = [send(10, rows(cr_in, 0, 8), rows(crh, PAD + 232, 8), -3),
               send(11, rows(cr_in, 288, 224), rows(crh, PAD + 8, 224), -2)]
    early = [send(12, rows(cs_in, 0, 56), rows(cs, PAD + 272, 56), 2),
             send(13, rows(cs_in, 384, 128), rows(cs, PAD + 144, 128), 3),
             send(14, rows(cs_in, 240 + RELAY, 144 - RELAY), rows(cs, PAD + RELAY, 144 - RELAY), 3)]
    straight = send(15, rows(cs_in, 240, RELAY), rows(cs, PAD, RELAY), 3)
    aside = send(16, rows(cs_in, 240, RELAY), relay, -1)
    onward = pltpu.make_async_remote_copy(
        src_ref=relay, dst_ref=rows(cs, PAD, RELAY), send_sem=send_sem.at[16], recv_sem=recv_sem.at[15],
        device_id=along(4), device_id_type=MESH)
    back = send(17, rows(cs_in, 56, 216), rows(cs, PAD + 328, 216), 2)
    odd = me[1] == 1
    sends = mortar_sends + halo_sends + [help_r[0], help_cr[0], help_r[1]] + early + [help_cr[1]]

    def mortar(index, piece, size, base, m, w):
        _, n, _, line, place = piece
        low, span = window(piece, size)

        def lanes(ref):
            row = ref[line : line + 1, :]
            return (pltpu.roll(row, 128 - place, 1) if place else row)[:, :n]

        spot, weights = lanes(m) - base, lanes(w)
        spot = jnp.where(spot < 0, spot + NROWS, spot)
        spot = jnp.where(spot >= NROWS, spot - NROWS, spot)
        row = lax.broadcasted_iota(jnp.int32, (span, n), 0) + low
        pt = jnp.where(row == spot, weights, 0.0) + jnp.where(row == spot + 1, 1.0 - weights, 0.0)
        give[index][...] = pt
        take[index][...] = jnp.transpose(pt)

    pl.semaphore_wait(barrier, len(greeted))
    pl.when(odd)(aside.start)
    for copy in sends:
        copy.start()
    pl.when(jnp.logical_not(odd))(straight.start)

    def spread(n):
        for offset in ((2, 0, 0, 0, 0), (10, 0, 0, 0, 0)):
            pl.semaphore_signal(token.at[n], inc=1, device_id=at(offset), device_id_type=MESH)

    spread(0)
    nothing = jnp.zeros((PAD, W), F32)
    for ref, size in ((u, EXT), (v, EXT), (v2, EXT), (uh, HELP), (vh, HELP), (vh2, HELP)):
        ref[0:PAD] = nothing
        ref[PAD + size : PAD + size + PAD] = nothing
    for ref in (im, se, se2, imh, seh):
        ref[...] = jnp.zeros(ref.shape, F32)
    own[0].wait()
    own[1].wait()
    for n, piece in enumerate(OWN):
        mortar(FIRST_OWN + n, piece, HELP, lax.rem(circ * ROWS + 1304, NROWS), m0, w0)

    col = lax.broadcasted_iota(jnp.int32, (1, W), 1)
    not_first = col > 0
    not_last = col < W - 1

    def around(ref, start, n):
        mid = ref[pl.ds(start, n)]
        beside = (jnp.where(not_first, pltpu.roll(mid, 1, 1), 0.0)
                  + jnp.where(not_last, pltpu.roll(mid, W - 1, 1), 0.0))
        return mid, 0.25 * (ref[pl.ds(start - 1, n)] + ref[pl.ds(start + 1, n)] + beside)

    def project(src, dst, index, piece, size):
        low, span = window(piece, size)
        dst[pl.ds(PAD + piece[0], piece[1])] = jnp.dot(
            take[index][...], src[pl.ds(PAD + low, span)], precision=HIGH, preferred_element_type=F32)

    def give_back(src, coef, dst, index, piece, size):
        low, span = window(piece, size)
        mid, rest = around(src, PAD + piece[0], piece[1])
        response = coef[pl.ds(PAD + piece[0], piece[1])] * mid - rest
        dst[pl.ds(PAD + low, span)] += jnp.dot(
            give[index][...], response, precision=HIGH, preferred_element_type=F32)

    def rotor_part(src, coef, dst, first, end):
        for start in range(first, end, 128):
            n = min(128, end - start)
            mid, rest = around(src, PAD + start, n)
            dst[pl.ds(PAD + start, n)] += coef[pl.ds(PAD + start, n)] * mid - rest

    def add_products(parts, b_ref, p_ref, s_ref, first, end):
        for start in range(first, end, 8):
            at_rows = pl.ds(PAD + start, 8)
            b, p, s = b_ref[at_rows], p_ref[at_rows], s_ref[at_rows]
            for n, product in enumerate((b * p, b * s, p * p, p * s, s * s)):
                parts[n] = parts[n] + product
        return parts

    pl.semaphore_wait(token.at[0], 2)
    spread(1)
    for copy in mortar_sends:
        copy.wait_recv()
    base = circ * ROWS - 16

    def prepare(n):
        piece = (FRONT + BACK)[n]
        mortar(n, piece, EXT, base, *((m3, w3) if piece[2] == 3 else (m2, w2)))

    for n in range(FIRST_BACK + 1):
        prepare(n)
    for copy in own[2:]:
        copy.wait()
    for copy in halo_sends:
        copy.wait_recv()
    for n in range(FIRST_BACK + 1):
        project(u, v, n, (FRONT + BACK)[n], EXT)
    rotor_part(u, cr, im, 8, 328)

    @pl.when(jnp.logical_not(odd))
    def _():
        aside.wait_recv()
        onward.start()

    back.start()
    pl.semaphore_wait(token.at[1], 2)
    for copy in help_r:
        copy.wait_recv()
    for n, piece in enumerate(OWN):
        project(uh, vh, FIRST_OWN + n, piece, HELP)
    for n, piece in enumerate(OWN):
        give_back(vh, csh, imh, FIRST_OWN + n, piece, HELP)

    def first(n):
        give_back(v, cs, im, n, FRONT[n], EXT)

    def look(n):
        project(im, v2, n, FRONT[n], EXT)

    def then(n):
        give_back(v2, cs, se, n, FRONT[n], EXT)

    early[0].wait_recv()
    first(4)
    early[1].wait_recv()
    first(2)
    first(3)
    look(4)
    look(3)
    look(2)
    rotor_part(im, cr, se, 168, 16 + CUT)
    then(4)
    then(3)
    parts = add_products([jnp.zeros((8, W), F32)] * 5, u, im, se, 168, 16 + CUT)
    for copy in help_cr:
        copy.wait_recv()
    rotor_part(uh, crh, imh, 8, 240)
    for n, piece in enumerate(OWN):
        project(imh, vh2, FIRST_OWN + n, piece, HELP)
    rotor_part(imh, crh, seh, 16, 232)
    for n, piece in enumerate(OWN):
        give_back(vh2, csh, seh, FIRST_OWN + n, piece, HELP)
    parts = add_products(parts, uh, imh, seh, 16, 232)

    early[2].wait_recv()
    straight.wait_recv()
    first(1)
    first(0)
    look(0)
    look(1)
    look(2)
    rotor_part(im, cr, se, 16, 168)
    then(0)
    then(1)
    then(2)
    parts = add_products(parts, u, im, se, 16, 168)

    lane = lax.broadcasted_iota(jnp.int32, (1, 128), 1)
    total = jnp.zeros((1, 128), F32)
    for n, part in enumerate(parts):
        line = jnp.sum(part[:, :128] + part[:, 128:], axis=0, keepdims=True)
        total = jnp.where(lane == n, jnp.sum(line, axis=1, keepdims=True), total)

    def late():
        for n in (FIRST_BACK + 1, FIRST_BACK + 2):
            prepare(n)
            project(u, v, n, (FRONT + BACK)[n], EXT)
        rotor_part(u, cr, im, 328, 536)
        back.wait_recv()
        for n, piece in enumerate(BACK):
            give_back(v, cs, im, FIRST_BACK + n, piece, EXT)
        for n, piece in list(enumerate(FRONT + BACK))[FIRST_BACK - 1 :]:
            project(im, v2, n, piece, EXT)
        rotor_part(im, cr, se2, 16 + CUT, 528)
        for n, piece in list(enumerate(FRONT + BACK))[FIRST_BACK - 1 :]:
            give_back(v2, cs, se2, n, piece, EXT)
        image_out[...] = im[PAD + 16 : PAD + 528]
        second_out[:CUT] = se[PAD + 16 : PAD + 16 + CUT]
        second_out[CUT:] = se2[PAD + 16 + CUT : PAD + 528]

    done = 0
    for stage, (partners, got) in enumerate(((X_PARTNERS, from_x), (Y_PARTNERS, from_y), (Z_PARTNERS, from_z))):
        mine[stage] = total
        copies = [
            pltpu.make_async_remote_copy(
                src_ref=mine.at[stage], dst_ref=got.at[pl.ds(n, 1)],
                send_sem=ar_send.at[done + n], recv_sem=ar_recv.at[done + n],
                device_id=at(offset), device_id_type=MESH)
            for n, offset in enumerate(partners)
        ]
        done += len(partners)
        for copy in copies:
            copy.start()
        if stage == 2:
            late()
        for copy in copies:
            copy.wait()
        total = total + jnp.sum(got[0 : len(partners)], axis=0, keepdims=True)

    def pick(n):
        return jnp.sum(jnp.where(lane == n, total, 0.0), axis=1, keepdims=True)

    cross_one, cross_two, gram_pp, gram_pq, gram_qq = [pick(n) for n in range(5)]
    determinant = gram_pp * gram_qq - gram_pq * gram_pq
    y1 = (gram_qq * cross_one - gram_pq * cross_two) / determinant
    y2 = (gram_pp * cross_two - gram_pq * cross_one) / determinant
    y1_out[...] = jnp.broadcast_to(y1, (1, W))
    y2_out[...] = jnp.broadcast_to(y2, (1, W))
    for copy in sends:
        copy.wait_send()
    back.wait_send()
    pl.when(odd)(aside.wait_send)

    @pl.when(jnp.logical_not(odd))
    def _():
        straight.wait_send()
        onward.wait_send()


def local(right_side, coef_rotor, coef_stator, mortar_rows, mortar_weight):
    main = pltpu.VMEM((PAD + EXT + PAD, W), F32)
    helper = pltpu.VMEM((PAD + HELP + PAD, W), F32)
    hbm = pl.BlockSpec(memory_space=pltpu.HBM)
    vmem = pl.BlockSpec(memory_space=pltpu.VMEM)
    image, second, y1, y2 = pl.pallas_call(
        kernel,
        out_shape=(pltpu.VMEM((ROWS, W), F32), pltpu.VMEM((ROWS, W), F32), pltpu.VMEM((1, W), F32), pltpu.VMEM((1, W), F32)),
        in_specs=[hbm] * 5,
        out_specs=(vmem,) * 4,
        scratch_shapes=[main] * 8
        + [helper] * 7
        + [pltpu.VMEM((RELAY, W), F32)]
        + [pltpu.VMEM((4, 128), jnp.int32)] * 3
        + [pltpu.VMEM((4, 128), F32)] * 3
        + [pltpu.VMEM((3, 1, 128), F32), pltpu.VMEM((8, 128), F32), pltpu.VMEM((8, 128), F32), pltpu.VMEM((16, 128), F32)]
        + [pltpu.SemaphoreType.DMA((n,)) for n in (5, N_SENDS, N_SENDS, 25, 25)]
        + [pltpu.SemaphoreType.REGULAR((2,))]
        + [pltpu.VMEM(s, F32) for s in SHAPES]
        + [pltpu.VMEM(s[::-1], F32) for s in SHAPES],
        compiler_params=pltpu.CompilerParams(collective_id=0, has_side_effects=True),
    )(right_side, coef_rotor, coef_stator, mortar_rows.reshape(4, 128), mortar_weight.reshape(4, 128))
    return y1 * right_side + y2 * image, right_side - y1 * image - y2 * second


def solution(mesh):
    finer = Mesh(mesh.devices.reshape(SIZES), AXES)
    circ, radax = AXES[:2], AXES[2:]
    whole = P(circ, radax)
    return jax.shard_map(local, mesh=finer, in_specs=(whole, whole, whole, P(circ), P(circ)),
                         out_specs=(whole, whole), check_vma=False)
```
